32 devices in a mesh: vid: 4 (over z), aud: 8 (over y, x, core).
Axes of the slice: x: 2, y: 2, z: 4, core: 2. Of those that a mesh axis runs over, the one named last changes fastest.
Arguments:
- video_tokens: bfloat16 [4096, 4096], P(('vid', 'aud')), may hold values from -28 to 28
- audio_tokens: bfloat16 [4096, 4096], P(('aud', 'vid')), may hold values from -28 to 28
- pair_weight: bfloat16 [4096, 256], replicated, may hold values from -0.125 to 0.125
- video_value: bfloat16 [4096, 256], replicated, may hold values from -0.125 to 0.125
- audio_value: bfloat16 [4096, 256], replicated, may hold values from -0.125 to 0.125
- video_output: bfloat16 [256, 4096], replicated, may hold values from -1 to 1
- audio_output: bfloat16 [256, 4096], replicated, may hold values from -1 to 1
- video_cotangent: bfloat16 [4096, 4096], P(('vid', 'aud')), may hold values from -0.59765625 to 0.59765625
- audio_cotangent: bfloat16 [4096, 4096], P(('aud', 'vid')), may hold values from -0.59765625 to 0.59765625
Outputs:
- video_result: bfloat16 [4096, 4096], P(('vid', 'aud'))
- audio_result: bfloat16 [4096, 4096], P(('aud', 'vid'))
- video_gradient: bfloat16 [4096, 4096], P(('vid', 'aud'))
- audio_gradient: bfloat16 [4096, 4096], P(('aud', 'vid'))
The draws below stay inside these ranges and needn't reach their ends.
All inputs are finite; a program needn't handle non-finite values.
Results may differ from the reference program's by a relative error of at most 0.015.
The reference program's roundings to bfloat16 on the way (of `score_grad`) count: a program that leaves them out, or rounds other values in their place, can miss the bound.
Values may be sent and summed in bfloat16 or wider, within the bound.
A program may use at most 192 MiB of HBM per device.

```python
import jax
import jax.numpy as jnp
from jax import lax

D = 4096
HS = 128
HEADS = 2
TV = 128
TA = 128
HD = 256
NV = 4096
NA = 4096
N_VID = 4
N_AUD = 8


def shared_rows(key):
    base_key = jax.random.fold_in(key, 11)
    key_video, key_audio = jax.random.split(base_key, 2)
    video_rows = jnp.clip(jax.random.normal(key_video, (NV, D), jnp.float32), -6.0, 6.0)
    audio_rows = jnp.clip(jax.random.normal(key_audio, (NA, D), jnp.float32), -6.0, 6.0)
    return (video_rows, audio_rows)


def draw_video_tokens(key, part):
    return shared_rows(key)[0].astype(jnp.bfloat16)


def draw_audio_tokens(key, part):
    return shared_rows(key)[1].astype(jnp.bfloat16)


def block_scale(own_key, extent, pieces, least, high):
    gain, own = 1.0, jax.random.fold_in(own_key, 6)
    for position, parts in pieces:
        draws = jnp.exp(jax.random.uniform(jax.random.fold_in(own, position), (parts,), jnp.float32, least / len(pieces), high / len(pieces)))
        gain = gain * jnp.repeat(draws, extent[position] // parts).reshape([-1 if axis == position else 1 for axis in range(len(extent))])
    return gain


def scatter_about(stream_key, dims, scale, limit, cuts=(), kind=jnp.bfloat16):
    level = block_scale(stream_key, dims, cuts, -0.22, 0.18) if cuts else 1.0
    drawn = jax.random.normal(stream_key, dims, jnp.float32) * scale * level
    return jnp.minimum(jnp.maximum(drawn, -limit), limit).astype(kind)


def setup_inputs(seed: int = 0) -> dict:
    arg_keys = jax.random.split(jax.random.key(seed), 10)
    video_tokens = draw_video_tokens(jax.random.fold_in(arg_keys[9], 71), 0)
    audio_tokens = draw_audio_tokens(jax.random.fold_in(arg_keys[9], 71), 0)
    pair_weight = scatter_about(arg_keys[2], (D, HD), (D // 2) ** -0.5, 0.125)
    video_value = scatter_about(arg_keys[3], (D, HD), (D // 2) ** -0.5, 0.125)
    audio_value = scatter_about(arg_keys[4], (D, HD), (D // 2) ** -0.5, 0.125)
    video_output = scatter_about(arg_keys[5], (HD, D), 0.2, 1.0)
    audio_output = scatter_about(arg_keys[6], (HD, D), 0.2, 1.0)
    video_cotangent = scatter_about(arg_keys[7], (NV, D), 0.1, 0.59765625, ((0, 32),))
    audio_cotangent = scatter_about(arg_keys[8], (NA, D), 0.1, 0.59765625, ((0, 32),))
    return {"video_tokens": video_tokens, "audio_tokens": audio_tokens, "pair_weight": pair_weight, "video_value": video_value, "audio_value": audio_value, "video_output": video_output, "audio_output": audio_output, "video_cotangent": video_cotangent, "audio_cotangent": audio_cotangent}


def tile_scores(left_rows, right_rows, score_scale):
    return score_scale * lax.dot_general(left_rows, right_rows, (((1,), (1,)), ((), ())), preferred_element_type=jnp.float32)


def rounded(values):
    return lax.optimization_barrier(values.astype(jnp.bfloat16)).astype(jnp.float32)


def blockwise(weights, right_rows, blocks, block_size, factor):
    left_part = weights.astype(jnp.float32).reshape(weights.shape[0], blocks, block_size)
    right_part = right_rows.astype(jnp.float32).reshape(blocks, block_size, right_rows.shape[1])
    partials = factor * jnp.einsum("vjk,jkh->jvh", left_part, right_part)
    return jnp.sum(rounded(partials), axis=0)


def transposed(weights, right_rows, factor):
    return rounded(factor * lax.dot_general(weights, right_rows, (((0,), (0,)), ((), ())), preferred_element_type=jnp.float32))


def reference(video_tokens, audio_tokens, pair_weight, video_value, audio_value, video_output, audio_output, video_cotangent, audio_cotangent):
    bf_type = jnp.bfloat16
    score_scale = float(HS) ** -0.5
    video_block = TV * N_AUD
    audio_block = TA * N_VID
    video_pairs = jnp.dot(video_tokens, pair_weight, preferred_element_type=jnp.float32).astype(bf_type)
    video_values = jnp.dot(video_tokens, video_value, preferred_element_type=jnp.float32).astype(bf_type)
    audio_pairs = jnp.dot(audio_tokens, pair_weight, preferred_element_type=jnp.float32).astype(bf_type)
    audio_values = jnp.dot(audio_tokens, audio_value, preferred_element_type=jnp.float32).astype(bf_type)
    contract_last = (((1,), (1,)), ((), ()))
    video_back = lax.dot_general(video_cotangent, video_output, contract_last, preferred_element_type=jnp.float32).astype(bf_type)
    audio_back = lax.dot_general(audio_cotangent, audio_output, contract_last, preferred_element_type=jnp.float32).astype(bf_type)
    video_mix_heads, audio_mix_heads = [], []
    video_pair_heads, video_value_heads, audio_pair_heads, audio_value_heads = [], [], [], []
    for head_index in range(HEADS):
        offset = head_index * HS
        head_vpairs = video_pairs[:, offset:offset + HS]
        head_apairs = audio_pairs[:, offset:offset + HS]
        head_vvalues = video_values[:, offset:offset + HS]
        head_avalues = audio_values[:, offset:offset + HS]
        head_vback = video_back[:, offset:offset + HS]
        head_aback = audio_back[:, offset:offset + HS]
        col_peak = jnp.full((NA,), -jnp.inf, jnp.float32)
        col_total = jnp.zeros((NA,), jnp.float32)
        for block_index in range(N_VID):
            first_row = block_index * video_block
            scores = tile_scores(head_vpairs[first_row:first_row + video_block], head_apairs, score_scale)
            new_peak = jnp.maximum(col_peak, jnp.max(scores, axis=0))
            col_total = col_total * jnp.exp(col_peak - new_peak) + jnp.sum(jnp.exp(scores - new_peak[None, :]), axis=0)
            col_peak = new_peak

        def probabilities(first_row):
            scores = tile_scores(head_vpairs[first_row:first_row + video_block], head_apairs, score_scale)
            row_exp = jnp.exp(scores - jnp.max(scores, axis=1, keepdims=True))
            row_prob = row_exp / jnp.sum(row_exp, axis=1, keepdims=True)
            col_prob = jnp.exp(scores - col_peak[None, :]) / col_total[None, :]
            return row_prob, col_prob

        video_mix_parts = []
        audio_mix_sum = jnp.zeros((NA, HS), jnp.float32)
        col_delta = jnp.zeros((NA,), jnp.float32)
        for block_index in range(N_VID):
            first_row = block_index * video_block
            row_prob, col_prob = probabilities(first_row)
            row_weight = row_prob.astype(bf_type)
            col_weight = col_prob.astype(bf_type)
            block_vvalues = head_vvalues[first_row:first_row + video_block]
            video_mix_parts.append(blockwise(row_weight, head_avalues, N_AUD, audio_block, 1.0))
            audio_mix_sum = audio_mix_sum + transposed(col_weight, block_vvalues, 1.0)
            col_grad = lax.dot_general(block_vvalues, head_aback, contract_last, preferred_element_type=jnp.float32)
            col_delta = col_delta + jnp.sum(col_prob * col_grad, axis=0)
        video_mix_heads.append(jnp.concatenate(video_mix_parts, axis=0))
        audio_mix_heads.append(audio_mix_sum)
        video_pair_parts, video_value_parts = [], []
        audio_pair_sum = jnp.zeros((NA, HS), jnp.float32)
        audio_value_sum = jnp.zeros((NA, HS), jnp.float32)
        for block_index in range(N_VID):
            first_row = block_index * video_block
            row_prob, col_prob = probabilities(first_row)
            row_weight = row_prob.astype(bf_type)
            col_weight = col_prob.astype(bf_type)
            block_vpairs = head_vpairs[first_row:first_row + video_block]
            block_vvalues = head_vvalues[first_row:first_row + video_block]
            block_vback = head_vback[first_row:first_row + video_block]
            row_grad = lax.dot_general(block_vback, head_avalues, contract_last, preferred_element_type=jnp.float32)
            col_grad = lax.dot_general(block_vvalues, head_aback, contract_last, preferred_element_type=jnp.float32)
            row_delta = jnp.sum(row_prob * row_grad, axis=1, keepdims=True)
            score_grad = (row_prob * (row_grad - row_delta) + col_prob * (col_grad - col_delta[None, :])).astype(bf_type)
            video_pair_parts.append(blockwise(score_grad, head_apairs, N_AUD, audio_block, score_scale))
            video_value_parts.append(blockwise(col_weight, head_aback, N_AUD, audio_block, 1.0))
            audio_pair_sum = audio_pair_sum + transposed(score_grad, block_vpairs, score_scale)
            audio_value_sum = audio_value_sum + transposed(row_weight, block_vback, 1.0)
        video_pair_heads.append(jnp.concatenate(video_pair_parts, axis=0))
        video_value_heads.append(jnp.concatenate(video_value_parts, axis=0))
        audio_pair_heads.append(audio_pair_sum)
        audio_value_heads.append(audio_value_sum)
    video_mix = jnp.concatenate(video_mix_heads, axis=1).astype(bf_type)
    audio_mix = jnp.concatenate(audio_mix_heads, axis=1).astype(bf_type)
    video_result = jnp.dot(video_mix, video_output, preferred_element_type=jnp.float32).astype(bf_type)
    audio_result = jnp.dot(audio_mix, audio_output, preferred_element_type=jnp.float32).astype(bf_type)
    video_pair_grad = jnp.concatenate(video_pair_heads, axis=1).astype(bf_type)
    video_value_grad = jnp.concatenate(video_value_heads, axis=1).astype(bf_type)
    audio_pair_grad = jnp.concatenate(audio_pair_heads, axis=1).astype(bf_type)
    audio_value_grad = jnp.concatenate(audio_value_heads, axis=1).astype(bf_type)
    video_gradient = (lax.dot_general(video_pair_grad, pair_weight, contract_last, preferred_element_type=jnp.float32)
                      + lax.dot_general(video_value_grad, video_value, contract_last, preferred_element_type=jnp.float32)).astype(bf_type)
    audio_gradient = (lax.dot_general(audio_pair_grad, pair_weight, contract_last, preferred_element_type=jnp.float32)
                      + lax.dot_general(audio_value_grad, audio_value, contract_last, preferred_element_type=jnp.float32)).astype(bf_type)
    return video_result, audio_result, video_gradient, audio_gradient
```

```python
import functools

import jax
import jax.numpy as jnp
from jax import lax
from jax.experimental import pallas as pl
from jax.experimental.pallas import tpu as pltpu
from jax.sharding import PartitionSpec as P

HS = 128
HEADS = 2
LANES = 128
MESH = pl.DeviceIdType.MESH
BF = jnp.bfloat16
F32 = jnp.float32


def product(left_side, right_side, left_dim, right_dim):
    return lax.dot_general(
        left_side,
        right_side,
        (((left_dim,), (right_dim,)), ((), ())),
        preferred_element_type=F32,
    )


def head_cols(head):
    return slice(head * HS, (head + 1) * HS)


def tile_kernel(
    n_vid,
    n_aud,
    vpairs_in,
    vvalues_in,
    vback_in,
    apairs_in,
    avalues_in,
    aback_in,
    vmix_out,
    vpair_out,
    vvalue_out,
    amix_out,
    apair_out,
    avalue_out,
    vblk,
    ablk,
    scores,
    colpeak,
    colsum,
    rstat,
    cstat,
    rfin,
    cfin,
    asum,
    vpart,
    vsib,
    vsum,
    vrecv,
    apart,
    arecv,
    vg_send,
    vg_recv,
    vf_send,
    vf_recv,
    ag_send,
    ag_recv,
    rs_send,
    rs_recv,
    cs_send,
    cs_recv,
    vs_send,
    vs_recv,
    vr_send,
    vr_recv,
    ar_send,
    ar_recv,
):
    scale = float(HS) ** -0.5
    vid, aud = lax.axis_index("vid"), lax.axis_index("aud")
    n_chip = n_aud // 2
    core = lax.rem(aud, 2)
    chip = aud // 2
    sibling = aud + 1 - 2 * core
    tv = vpairs_in.shape[0]
    ta = apairs_in.shape[0]
    na = n_vid * ta

    barrier = pltpu.get_barrier_semaphore()
    for d in range(1, n_aud):
        pl.semaphore_signal(
            barrier, inc=1, device_id={"aud": lax.rem(aud + d, n_aud)}, device_id_type=MESH
        )
    for d in range(1, n_vid):
        pl.semaphore_signal(
            barrier, inc=1, device_id={"vid": lax.rem(vid + d, n_vid)}, device_id_type=MESH
        )
    pl.semaphore_wait(barrier, n_aud + n_vid - 2)

    def remote(src, dst, send, recv, where):
        return pltpu.make_async_remote_copy(
            src_ref=src,
            dst_ref=dst,
            send_sem=send,
            recv_sem=recv,
            device_id=where,
            device_id_type=MESH,
        )

    pending = []

    def launch(copy):
        copy.start()
        pending.append(copy)
        return copy

    v_in = (vpairs_in, vvalues_in, vback_in)
    a_in = (apairs_in, avalues_in, aback_in)
    a_copies, v_copies, s_copies = {}, {}, {}
    for p in range(3):
        for d in range(1, n_vid):
            a_copies[p, d] = launch(
                remote(
                    a_in[p],
                    ablk.at[p, vid],
                    ag_send.at[p, d],
                    ag_recv.at[p, d],
                    {"vid": lax.rem(vid + d, n_vid)},
                )
            )
        for d in range(1, n_chip):
            v_copies[p, d] = launch(
                remote(
                    v_in[p],
                    vblk.at[p, aud],
                    vg_send.at[p, d],
                    vg_recv.at[p, d],
                    {"aud": lax.rem(aud + 2 * d, n_aud)},
                )
            )
        s_copies[p, 0] = launch(
            remote(
                v_in[p], vblk.at[p, aud], vf_send.at[p, 0], vf_recv.at[p, 0], {"aud": sibling}
            )
        )
    for p in range(3):
        vblk[p, aud] = v_in[p][...]
        ablk[p, vid] = a_in[p][...]

    def finish_gather(p):
        for d in range(1, n_chip):
            v_copies[p, d].wait_recv()
            owner = lax.rem(aud + n_aud - 2 * d, n_aud)
            s_copies[p, d] = launch(
                remote(
                    vblk.at[p, owner],
                    vblk.at[p, owner],
                    vf_send.at[p, d],
                    vf_recv.at[p, d],
                    {"aud": sibling},
                )
            )
        for d in range(n_chip):
            s_copies[p, d].wait_recv()
        for d in range(1, n_vid):
            a_copies[p, d].wait_recv()

    def audio_side(p, head):
        return ablk[p, :, :, head_cols(head)].reshape(na, HS)

    finish_gather(0)
    for head in range(HEADS):
        apairs = audio_side(0, head)
        colpeak[head] = jnp.full((8, na), -jnp.inf, F32)

        def score_step(i, carry, head=head, apairs=apairs):
            s = scale * product(vblk[0, i, :, head_cols(head)], apairs, 1, 1)
            scores[head, i] = s
            colpeak[head] = jnp.maximum(
                colpeak[head], jnp.max(s.reshape(tv // 8, 8, na), axis=0)
            )
            return carry

        lax.fori_loop(0, n_aud, score_step, 0)
    finish_gather(1)
    finish_gather(2)

    lane = lax.broadcasted_iota(jnp.int32, (tv, LANES), 1)
    sub = lax.broadcasted_iota(jnp.int32, (LANES, tv), 0)
    stat_copies = {0: [], 1: []}
    for head in range(HEADS):
        avalues, aback = audio_side(1, head), audio_side(2, head)
        peak = jnp.max(colpeak[head], axis=0, keepdims=True)
        colsum[...] = jnp.zeros_like(colsum)

        def stat_step(i, carry, head=head, avalues=avalues, aback=aback, peak=peak):
            s = scores[head, i]
            row_peak = jnp.max(s, axis=1, keepdims=True)
            row_exp = jnp.exp(s - row_peak)
            col_exp = jnp.exp(s - peak)
            row_grad = product(vblk[2, i, :, head_cols(head)], avalues, 1, 1)
            col_grad = product(vblk[1, i, :, head_cols(head)], aback, 1, 1)
            row_total = jnp.sum(row_exp, axis=1, keepdims=True)
            row_dot = jnp.sum(row_exp * row_grad, axis=1, keepdims=True)
            colsum[0] += jnp.sum(col_exp.reshape(tv // 8, 8, na), axis=0)
            colsum[1] += jnp.sum((col_exp * col_grad).reshape(tv // 8, 8, na), axis=0)
            packed = jnp.where(lane == 0, row_peak, jnp.where(lane == 1, row_total, row_dot)).T
            for k in range(3):
                rstat[head, 0, k, pl.ds(i, 1), :] = packed[k : k + 1]
            return carry

        lax.fori_loop(0, n_aud, stat_step, 0)
        cstat[head, 0, 0:1] = peak
        for k in range(2):
            cstat[head, 0, k + 1 : k + 2] = jnp.sum(colsum[k], axis=0, keepdims=True)
        for d in range(1, n_aud):
            stat_copies[head].append(
                launch(
                    remote(
                        rstat.at[head, 0],
                        rstat.at[head, d],
                        rs_send.at[head, d],
                        rs_recv.at[head, d],
                        {"aud": lax.rem(aud + d, n_aud)},
                    )
                )
            )
        for d in range(1, n_vid):
            stat_copies[head].append(
                launch(
                    remote(
                        cstat.at[head, 0],
                        cstat.at[head, d],
                        cs_send.at[head, d],
                        cs_recv.at[head, d],
                        {"vid": lax.rem(vid + d, n_vid)},
                    )
                )
            )

    def combine(parts):
        top = functools.reduce(jnp.maximum, [part[0] for part in parts])
        gains = [jnp.exp(part[0] - top) for part in parts]
        total = sum(part[1] * gain for part, gain in zip(parts, gains))
        dots = sum(part[2] * gain for part, gain in zip(parts, gains))
        return top, 1.0 / total, dots / total

    sib_copies, vr_copies, ar_copies = {}, {}, {}

    def reduce_video(head):
        sib_copies[head].wait_recv()
        for d in range(1, n_chip):
            peer = lax.rem(chip + d, n_chip)
            vsum[head, d] = (
                vpart[head, core, peer].astype(F32) + vsib[head, peer].astype(F32)
            ).astype(BF)
            vr_copies[head, d] = launch(
                remote(
                    vsum.at[head, d],
                    vrecv.at[head, d],
                    vr_send.at[head, d],
                    vr_recv.at[head, d],
                    {"aud": lax.rem(aud + 2 * d, n_aud)},
                )
            )

    for head in range(HEADS):
        for copy in stat_copies[head]:
            copy.wait_recv()
        for k, value in enumerate(
            combine([[rstat[head, d, k] for k in range(3)] for d in range(n_aud)])
        ):
            rfin[k] = value
        for k, value in enumerate(
            combine([[cstat[head, d, k : k + 1] for k in range(3)] for d in range(n_vid)])
        ):
            cfin[k : k + 1] = value
        apairs, avalues, aback = (audio_side(p, head) for p in range(3))
        asum[...] = jnp.zeros_like(asum)

        def grad_step(i, carry, head=head, apairs=apairs, avalues=avalues, aback=aback):
            rows = [rfin[k, pl.ds(i, 1), :] for k in range(3)]
            back = jnp.where(sub == 0, rows[0], jnp.where(sub == 1, rows[1], rows[2])).T
            s = scores[head, i]
            vpairs = vblk[0, i, :, head_cols(head)]
            vvalues = vblk[1, i, :, head_cols(head)]
            vback = vblk[2, i, :, head_cols(head)]
            row_prob = jnp.exp(s - back[:, 0:1]) * back[:, 1:2]
            col_prob = jnp.exp(s - cfin[0:1]) * cfin[1:2]
            row_weight, col_weight = row_prob.astype(BF), col_prob.astype(BF)
            row_grad = product(vback, avalues, 1, 1)
            col_grad = product(vvalues, aback, 1, 1)
            score_grad = (
                row_prob * (row_grad - back[:, 2:3]) + col_prob * (col_grad - cfin[2:3])
            ).astype(BF)
            slot = (head, lax.rem(i, 2), i // 2)
            vpart[slot + (slice(None), slice(0, HS))] = product(row_weight, avalues, 1, 0).astype(BF)
            vpart[slot + (slice(None), slice(HS, 2 * HS))] = (
                scale * product(score_grad, apairs, 1, 0)
            ).astype(BF)
            vpart[slot + (slice(None), slice(2 * HS, 3 * HS))] = product(
                col_weight, aback, 1, 0
            ).astype(BF)
            asum[:, 0:HS] += product(col_weight, vvalues, 0, 0)
            asum[:, HS : 2 * HS] += product(score_grad, vpairs, 0, 0)
            asum[:, 2 * HS : 3 * HS] += product(row_weight, vback, 0, 0)
            return carry

        lax.fori_loop(0, n_aud, grad_step, 0)
        for t in range(n_vid):
            rows = slice(t * ta, (t + 1) * ta)
            apart[head, t, :, 0:HS] = asum[rows, 0:HS].astype(BF)
            apart[head, t, :, HS : 2 * HS] = (scale * asum[rows, HS : 2 * HS]).astype(BF)
            apart[head, t, :, 2 * HS : 3 * HS] = asum[rows, 2 * HS : 3 * HS].astype(BF)
        for d in range(1, n_vid):
            peer = lax.rem(vid + d, n_vid)
            ar_copies[head, d] = launch(
                remote(
                    apart.at[head, peer],
                    arecv.at[head, d],
                    ar_send.at[head, d],
                    ar_recv.at[head, d],
                    {"vid": peer},
                )
            )
        sib_copies[head] = launch(
            remote(
                vpart.at[head, 1 - core],
                vsib.at[head],
                vs_send.at[head],
                vs_recv.at[head],
                {"aud": sibling},
            )
        )
        if head > 0:
            reduce_video(head - 1)
    reduce_video(HEADS - 1)

    v_out = (vmix_out, vpair_out, vvalue_out)
    a_out = (amix_out, apair_out, avalue_out)
    for head in range(HEADS):
        for d in range(1, n_chip):
            vr_copies[head, d].wait_recv()
        total = vpart[head, core, chip].astype(F32) + vsib[head, chip].astype(F32)
        for d in range(1, n_chip):
            total += vrecv[head, d].astype(F32)
        for k in range(3):
            v_out[k][:, head_cols(head)] = total[:, head_cols(k)].astype(BF)
        for d in range(1, n_vid):
            ar_copies[head, d].wait_recv()
        total = apart[head, vid].astype(F32)
        for d in range(1, n_vid):
            total += arecv[head, d].astype(F32)
        for k in range(3):
            a_out[k][:, head_cols(head)] = total[:, head_cols(k)].astype(BF)
    for copy in pending:
        copy.wait_send()


def attention_tile(n_vid, n_aud, tv, ta, arrays):
    nv, na = n_aud * tv, n_vid * ta
    n_chip = n_aud // 2
    hd = HEADS * HS
    wide = 3 * HS
    dma = pltpu.SemaphoreType.DMA
    v_shape = jax.ShapeDtypeStruct((tv, hd), BF)
    a_shape = jax.ShapeDtypeStruct((ta, hd), BF)
    sems = [
        (3, n_chip),
        (3, n_chip),
        (3, n_vid),
        (HEADS, n_aud),
        (HEADS, n_vid),
        (HEADS,),
        (HEADS, n_chip),
        (HEADS, n_vid),
    ]
    return pl.pallas_call(
        functools.partial(tile_kernel, n_vid, n_aud),
        out_shape=(v_shape,) * 3 + (a_shape,) * 3,
        in_specs=[pl.BlockSpec(memory_space=pltpu.VMEM)] * 6,
        out_specs=(pl.BlockSpec(memory_space=pltpu.VMEM),) * 6,
        scratch_shapes=[
            pltpu.VMEM((3, n_aud, tv, hd), BF),
            pltpu.VMEM((3, n_vid, ta, hd), BF),
            pltpu.VMEM((HEADS, n_aud, tv, na), F32),
            pltpu.VMEM((HEADS, 8, na), F32),
            pltpu.VMEM((2, 8, na), F32),
            pltpu.VMEM((HEADS, n_aud, 3, n_aud, LANES), F32),
            pltpu.VMEM((HEADS, n_vid, 3, na), F32),
            pltpu.VMEM((3, n_aud, LANES), F32),
            pltpu.VMEM((3, na), F32),
            pltpu.VMEM((na, wide), F32),
            pltpu.VMEM((HEADS, 2, n_chip, tv, wide), BF),
            pltpu.VMEM((HEADS, n_chip, tv, wide), BF),
            pltpu.VMEM((HEADS, n_chip, tv, wide), BF),
            pltpu.VMEM((HEADS, n_chip, tv, wide), BF),
            pltpu.VMEM((HEADS, n_vid, ta, wide), BF),
            pltpu.VMEM((HEADS, n_vid, ta, wide), BF),
        ]
        + [dma(shape) for shape in sems for _ in range(2)],
        compiler_params=pltpu.CompilerParams(
            collective_id=0, has_side_effects=True, vmem_limit_bytes=52 * 1024 * 1024
        ),
    )(*arrays)


def on_device(
    n_vid,
    n_aud,
    video_tokens,
    audio_tokens,
    pair_weight,
    video_value,
    audio_value,
    video_output,
    audio_output,
    video_cotangent,
    audio_cotangent,
):
    projected = (
        product(video_tokens, pair_weight, 1, 0).astype(BF),
        product(video_tokens, video_value, 1, 0).astype(BF),
        product(video_cotangent, video_output, 1, 1).astype(BF),
        product(audio_tokens, pair_weight, 1, 0).astype(BF),
        product(audio_tokens, audio_value, 1, 0).astype(BF),
        product(audio_cotangent, audio_output, 1, 1).astype(BF),
    )
    vmix, vpair, vvalue, amix, apair, avalue = attention_tile(
        n_vid, n_aud, video_tokens.shape[0], audio_tokens.shape[0], projected
    )
    video_result = product(vmix, video_output, 1, 0).astype(BF)
    audio_result = product(amix, audio_output, 1, 0).astype(BF)
    video_gradient = (
        product(vpair, pair_weight, 1, 1) + product(vvalue, video_value, 1, 1)
    ).astype(BF)
    audio_gradient = (
        product(apair, pair_weight, 1, 1) + product(avalue, audio_value, 1, 1)
    ).astype(BF)
    return (video_result, audio_result, video_gradient, audio_gradient)


def solution(mesh):
    rows_v, rows_a = P(("vid", "aud"), None), P(("aud", "vid"), None)
    return jax.shard_map(
        functools.partial(on_device, mesh.shape["vid"], mesh.shape["aud"]),
        mesh=mesh,
        in_specs=(rows_v, rows_a, P(), P(), P(), P(), P(), rows_v, rows_a),
        out_specs=(rows_v, rows_a, rows_v, rows_a),
        check_vma=False,
    )
```

```python
import functools

import jax
import jax.numpy as jnp
from jax import lax
from jax.experimental import pallas as pl
from jax.experimental.pallas import tpu as pltpu
from jax.sharding import PartitionSpec as P

HS = 128
HEADS = 2
LANES = 128
MESH = pl.DeviceIdType.MESH
BF = jnp.bfloat16
F32 = jnp.float32


def product(left_side, right_side, left_dim, right_dim):
    return lax.dot_general(
        left_side,
        right_side,
        (((left_dim,), (right_dim,)), ((), ())),
        preferred_element_type=F32,
    )


def head_cols(head):
    return slice(head * HS, (head + 1) * HS)


def tile_kernel(
    n_vid,
    n_aud,
    vt_hbm,
    at_hbm,
    pw_hbm,
    vv_hbm,
    av_hbm,
    vo_hbm,
    ao_hbm,
    vc_hbm,
    ac_hbm,
    vmix_out,
    vpair_out,
    vvalue_out,
    amix_out,
    apair_out,
    avalue_out,
    vt,
    at,
    pw,
    vv,
    av,
    vo,
    ao,
    vc,
    ac,
    vblk,
    ablk,
    scores,
    colpeak,
    colsum,
    rstat,
    cstat,
    rfin,
    cfin,
    asum,
    vpart,
    vsib,
    vsum,
    vrecv,
    apart,
    arecv,
    load_sem,
    vg_send,
    vg_recv,
    vf_send,
    vf_recv,
    ag_send,
    ag_recv,
    rs_send,
    rs_recv,
    cs_send,
    cs_recv,
    vs_send,
    vs_recv,
    vr_send,
    vr_recv,
    ar_send,
    ar_recv,
):
    scale = float(HS) ** -0.5
    vid, aud = lax.axis_index("vid"), lax.axis_index("aud")
    n_chip = n_aud // 2
    core = lax.rem(aud, 2)
    chip = aud // 2
    sibling = aud + 1 - 2 * core
    tv, ta = vt.shape[0], at.shape[0]
    na = n_vid * ta

    loads = {}
    for k, (name, src, dst) in enumerate(
        (
            ("at", at_hbm, at),
            ("pw", pw_hbm, pw),
            ("av", av_hbm, av),
            ("ac", ac_hbm, ac),
            ("ao", ao_hbm, ao),
            ("vt", vt_hbm, vt),
            ("vv", vv_hbm, vv),
            ("vc", vc_hbm, vc),
            ("vo", vo_hbm, vo),
        )
    ):
        loads[name] = pltpu.make_async_copy(src, dst, load_sem.at[k])
        loads[name].start()

    barrier = pltpu.get_barrier_semaphore()
    for d in range(1, n_aud):
        pl.semaphore_signal(
            barrier, inc=1, device_id={"aud": lax.rem(aud + d, n_aud)}, device_id_type=MESH
        )
    for d in range(1, n_vid):
        pl.semaphore_signal(
            barrier, inc=1, device_id={"vid": lax.rem(vid + d, n_vid)}, device_id_type=MESH
        )

    def remote(src, dst, send, recv, where):
        return pltpu.make_async_remote_copy(
            src_ref=src,
            dst_ref=dst,
            send_sem=send,
            recv_sem=recv,
            device_id=where,
            device_id_type=MESH,
        )

    pending = []

    def launch(copy):
        copy.start()
        pending.append(copy)
        return copy

    def project(blk, owner, p, left, right, right_dim):
        full = product(left[...], right[...], 1, right_dim).astype(BF)
        for head in range(HEADS):
            blk[head, owner, p] = full[:, head_cols(head)]

    def hop(head, way, s):
        owner = vid - s + 1 if way == 0 else vid + s - 1
        return remote(
            ablk.at[head, owner],
            ablk.at[head, owner],
            ag_send.at[head, way, s],
            ag_recv.at[head, way, s],
            {"vid": vid + 1 if way == 0 else vid - 1},
        )

    def sends(way, s):
        if way == 0:
            return (vid + 1 < n_vid) & (vid - s + 1 >= 0)
        return (vid > 0) & (vid + s - 1 < n_vid)

    def arrives(way, s):
        return vid - s >= 0 if way == 0 else vid + s < n_vid

    def audio_hop(head, s):
        for way in range(2):

            @pl.when(sends(way, s))
            def _(way=way):
                hop(head, way, s).start()

    def audio_take(head, s):
        for way in range(2):

            @pl.when(arrives(way, s))
            def _(way=way):
                hop(head, way, s).wait_recv()

        if s + 1 < n_vid:
            audio_hop(head, s + 1)

    loads["at"].wait()
    loads["pw"].wait()
    project(ablk, vid, 0, at, pw, 0)
    loads["av"].wait()
    project(ablk, vid, 1, at, av, 0)
    loads["ac"].wait()
    loads["ao"].wait()
    project(ablk, vid, 2, ac, ao, 1)
    pl.semaphore_wait(barrier, n_aud + n_vid - 2)
    for head in range(HEADS):
        audio_hop(head, 1)
    loads["vt"].wait()
    project(vblk, aud, 0, vt, pw, 0)
    loads["vv"].wait()
    project(vblk, aud, 1, vt, vv, 0)
    loads["vc"].wait()
    loads["vo"].wait()
    project(vblk, aud, 2, vc, vo, 1)
    v_copies, s_copies = {}, {}

    def share_own(head):
        for d in range(1, n_chip):
            v_copies[head, d] = launch(
                remote(
                    vblk.at[head, aud],
                    vblk.at[head, aud],
                    vg_send.at[head, d],
                    vg_recv.at[head, d],
                    {"aud": lax.rem(aud + 2 * d, n_aud)},
                )
            )
        s_copies[head, 0] = launch(
            remote(
                vblk.at[head, aud],
                vblk.at[head, aud],
                vf_send.at[head, 0],
                vf_recv.at[head, 0],
                {"aud": sibling},
            )
        )

    def video_take(head):
        for d in range(1, n_chip):
            v_copies[head, d].wait_recv()
            owner = lax.rem(aud + n_aud - 2 * d, n_aud)
            s_copies[head, d] = launch(
                remote(
                    vblk.at[head, owner],
                    vblk.at[head, owner],
                    vf_send.at[head, d],
                    vf_recv.at[head, d],
                    {"aud": sibling},
                )
            )

    def video_done(head):
        for d in range(n_chip):
            s_copies[head, d].wait_recv()

    def audio_side(p, head):
        return ablk[head, :, p].reshape(na, HS)

    for head in range(HEADS):
        share_own(head)
    audio_take(0, 1)
    video_take(0)
    for s in range(2, n_vid):
        audio_take(0, s)
    video_done(0)

    lane = lax.broadcasted_iota(jnp.int32, (tv, LANES), 1)
    sub = lax.broadcasted_iota(jnp.int32, (LANES, tv), 0)
    stat_copies = {0: [], 1: []}
    for head in range(HEADS):
        apairs, avalues, aback = (audio_side(p, head) for p in range(3))
        colpeak[head] = jnp.full((8, na), -jnp.inf, F32)

        def score_step(i, carry, head=head, apairs=apairs):
            s = scale * product(vblk[head, i, 0], apairs, 1, 1)
            scores[head, i] = s
            colpeak[head] = jnp.maximum(
                colpeak[head], jnp.max(s.reshape(tv // 8, 8, na), axis=0)
            )
            return carry

        lax.fori_loop(0, n_aud, score_step, 0)
        if head + 1 < HEADS:
            audio_take(head + 1, 1)
            video_take(head + 1)
        peak = jnp.max(colpeak[head], axis=0, keepdims=True)
        colsum[...] = jnp.zeros_like(colsum)

        def stat_step(i, carry, head=head, avalues=avalues, aback=aback, peak=peak):
            s = scores[head, i]
            row_peak = jnp.max(s, axis=1, keepdims=True)
            row_exp = jnp.exp(s - row_peak)
            col_exp = jnp.exp(s - peak)
            row_grad = product(vblk[head, i, 2], avalues, 1, 1)
            col_grad = product(vblk[head, i, 1], aback, 1, 1)
            row_total = jnp.sum(row_exp, axis=1, keepdims=True)
            row_dot = jnp.sum(row_exp * row_grad, axis=1, keepdims=True)
            colsum[0] += jnp.sum(col_exp.reshape(tv // 8, 8, na), axis=0)
            colsum[1] += jnp.sum((col_exp * col_grad).reshape(tv // 8, 8, na), axis=0)
            packed = jnp.where(lane == 0, row_peak, jnp.where(lane == 1, row_total, row_dot)).T
            for k in range(3):
                rstat[head, 0, k, pl.ds(i, 1), :] = packed[k : k + 1]
            return carry

        if head + 1 < HEADS:
            steps = max(n_vid - 2, 1)
            for k in range(steps):
                lax.fori_loop(k * n_aud // steps, (k + 1) * n_aud // steps, stat_step, 0)
                if k + 2 < n_vid:
                    audio_take(head + 1, k + 2)
        else:
            lax.fori_loop(0, n_aud, stat_step, 0)
        cstat[head, 0, 0:1] = peak
        for k in range(2):
            cstat[head, 0, k + 1 : k + 2] = jnp.sum(colsum[k], axis=0, keepdims=True)
        for d in range(1, n_aud):
            stat_copies[head].append(
                launch(
                    remote(
                        rstat.at[head, 0],
                        rstat.at[head, d],
                        rs_send.at[head, d],
                        rs_recv.at[head, d],
                        {"aud": lax.rem(aud + d, n_aud)},
                    )
                )
            )
        for d in range(1, n_vid):
            stat_copies[head].append(
                launch(
                    remote(
                        cstat.at[head, 0],
                        cstat.at[head, d],
                        cs_send.at[head, d],
                        cs_recv.at[head, d],
                        {"vid": lax.rem(vid + d, n_vid)},
                    )
                )
            )

        if head + 1 < HEADS:
            video_done(head + 1)

    def combine(parts):
        top = functools.reduce(jnp.maximum, [part[0] for part in parts])
        gains = [jnp.exp(part[0] - top) for part in parts]
        total = sum(part[1] * gain for part, gain in zip(parts, gains))
        dots = sum(part[2] * gain for part, gain in zip(parts, gains))
        return top, 1.0 / total, dots / total

    sib_copies, vr_copies, ar_copies = {}, {}, {}

    def reduce_video(head):
        sib_copies[head].wait_recv()
        for d in range(1, n_chip):
            peer = lax.rem(chip + d, n_chip)
            vsum[head, d] = (
                vpart[head, core, peer].astype(F32) + vsib[head, peer].astype(F32)
            ).astype(BF)
            vr_copies[head, d] = launch(
                remote(
                    vsum.at[head, d],
                    vrecv.at[head, d],
                    vr_send.at[head, d],
                    vr_recv.at[head, d],
                    {"aud": lax.rem(aud + 2 * d, n_aud)},
                )
            )

    for head in range(HEADS):
        for copy in stat_copies[head]:
            copy.wait_recv()
        for k, value in enumerate(
            combine([[rstat[head, d, k] for k in range(3)] for d in range(n_aud)])
        ):
            rfin[k] = value
        for k, value in enumerate(
            combine([[cstat[head, d, k : k + 1] for k in range(3)] for d in range(n_vid)])
        ):
            cfin[k : k + 1] = value
        apairs, avalues, aback = (audio_side(p, head) for p in range(3))
        asum[...] = jnp.zeros_like(asum)

        def grad_step(i, carry, head=head, apairs=apairs, avalues=avalues, aback=aback):
            rows = [rfin[k, pl.ds(i, 1), :] for k in range(3)]
            back = jnp.where(sub == 0, rows[0], jnp.where(sub == 1, rows[1], rows[2])).T
            s = scores[head, i]
            vpairs = vblk[head, i, 0]
            vvalues = vblk[head, i, 1]
            vback = vblk[head, i, 2]
            row_prob = jnp.exp(s - back[:, 0:1]) * back[:, 1:2]
            col_prob = jnp.exp(s - cfin[0:1]) * cfin[1:2]
            row_weight, col_weight = row_prob.astype(BF), col_prob.astype(BF)
            row_grad = product(vback, avalues, 1, 1)
            col_grad = product(vvalues, aback, 1, 1)
            score_grad = (
                row_prob * (row_grad - back[:, 2:3]) + col_prob * (col_grad - cfin[2:3])
            ).astype(BF)
            slot = (head, lax.rem(i, 2), i // 2)
            vpart[slot + (slice(None), slice(0, HS))] = product(row_weight, avalues, 1, 0).astype(BF)
            vpart[slot + (slice(None), slice(HS, 2 * HS))] = (
                scale * product(score_grad, apairs, 1, 0)
            ).astype(BF)
            vpart[slot + (slice(None), slice(2 * HS, 3 * HS))] = product(
                col_weight, aback, 1, 0
            ).astype(BF)
            asum[:, 0:HS] += product(col_weight, vvalues, 0, 0)
            asum[:, HS : 2 * HS] += product(score_grad, vpairs, 0, 0)
            asum[:, 2 * HS : 3 * HS] += product(row_weight, vback, 0, 0)
            return carry

        lax.fori_loop(0, n_aud, grad_step, 0)
        for t in range(n_vid):
            rows = slice(t * ta, (t + 1) * ta)
            apart[head, t, :, 0:HS] = asum[rows, 0:HS].astype(BF)
            apart[head, t, :, HS : 2 * HS] = (scale * asum[rows, HS : 2 * HS]).astype(BF)
            apart[head, t, :, 2 * HS : 3 * HS] = asum[rows, 2 * HS : 3 * HS].astype(BF)
        for d in range(1, n_vid):
            peer = lax.rem(vid + d, n_vid)
            ar_copies[head, d] = launch(
                remote(
                    apart.at[head, peer],
                    arecv.at[head, d],
                    ar_send.at[head, d],
                    ar_recv.at[head, d],
                    {"vid": peer},
                )
            )
        sib_copies[head] = launch(
            remote(
                vpart.at[head, 1 - core],
                vsib.at[head],
                vs_send.at[head],
                vs_recv.at[head],
                {"aud": sibling},
            )
        )
        if head > 0:
            reduce_video(head - 1)
    reduce_video(HEADS - 1)

    v_out = (vmix_out, vpair_out, vvalue_out)
    a_out = (amix_out, apair_out, avalue_out)
    for head in range(HEADS):
        for d in range(1, n_chip):
            vr_copies[head, d].wait_recv()
        total = vpart[head, core, chip].astype(F32) + vsib[head, chip].astype(F32)
        for d in range(1, n_chip):
            total += vrecv[head, d].astype(F32)
        for k in range(3):
            v_out[k][:, head_cols(head)] = total[:, head_cols(k)].astype(BF)
        for d in range(1, n_vid):
            ar_copies[head, d].wait_recv()
        total = apart[head, vid].astype(F32)
        for d in range(1, n_vid):
            total += arecv[head, d].astype(F32)
        for k in range(3):
            a_out[k][:, head_cols(head)] = total[:, head_cols(k)].astype(BF)
    for head in range(HEADS):
        for way in range(2):
            for s in range(1, n_vid):

                @pl.when(sends(way, s))
                def _(head=head, way=way, s=s):
                    hop(head, way, s).wait_send()

    for copy in pending:
        copy.wait_send()


def attention_tile(n_vid, n_aud, tv, ta, arrays):
    nv, na = n_aud * tv, n_vid * ta
    n_chip = n_aud // 2
    wide = 3 * HS
    dma = pltpu.SemaphoreType.DMA
    v_shape = jax.ShapeDtypeStruct((tv, HEADS * HS), BF)
    a_shape = jax.ShapeDtypeStruct((ta, HEADS * HS), BF)
    sems = [
        (HEADS, n_chip),
        (HEADS, n_chip),
        (HEADS, 2, n_vid),
        (HEADS, n_aud),
        (HEADS, n_vid),
        (HEADS,),
        (HEADS, n_chip),
        (HEADS, n_vid),
    ]
    return pl.pallas_call(
        functools.partial(tile_kernel, n_vid, n_aud),
        out_shape=(v_shape,) * 3 + (a_shape,) * 3,
        in_specs=[pl.BlockSpec(memory_space=pl.ANY)] * 9,
        out_specs=(pl.BlockSpec(memory_space=pltpu.VMEM),) * 6,
        scratch_shapes=[pltpu.VMEM(array.shape, BF) for array in arrays]
        + [
            pltpu.VMEM((HEADS, n_aud, 3, tv, HS), BF),
            pltpu.VMEM((HEADS, n_vid, 3, ta, HS), BF),
            pltpu.VMEM((HEADS, n_aud, tv, na), F32),
            pltpu.VMEM((HEADS, 8, na), F32),
            pltpu.VMEM((2, 8, na), F32),
            pltpu.VMEM((HEADS, n_aud, 3, n_aud, LANES), F32),
            pltpu.VMEM((HEADS, n_vid, 3, na), F32),
            pltpu.VMEM((3, n_aud, LANES), F32),
            pltpu.VMEM((3, na), F32),
            pltpu.VMEM((na, wide), F32),
            pltpu.VMEM((HEADS, 2, n_chip, tv, wide), BF),
            pltpu.VMEM((HEADS, n_chip, tv, wide), BF),
            pltpu.VMEM((HEADS, n_chip, tv, wide), BF),
            pltpu.VMEM((HEADS, n_chip, tv, wide), BF),
            pltpu.VMEM((HEADS, n_vid, ta, wide), BF),
            pltpu.VMEM((HEADS, n_vid, ta, wide), BF),
        ]
        + [dma((len(arrays),))]
        + [dma(shape) for shape in sems for _ in range(2)],
        compiler_params=pltpu.CompilerParams(
            collective_id=0, has_side_effects=True, vmem_limit_bytes=63 * 1024 * 1024
        ),
    )(*arrays)


def expand_kernel(
    vmix, vpair, vvalue, amix, apair, avalue, pw, vv, av, vo, ao, vres, ares, vgrad, agrad
):
    vres[...] = product(vmix[...], vo[...], 1, 0).astype(BF)
    ares[...] = product(amix[...], ao[...], 1, 0).astype(BF)
    vgrad[...] = (
        product(vpair[...], pw[...], 1, 1) + product(vvalue[...], vv[...], 1, 1)
    ).astype(BF)
    agrad[...] = (
        product(apair[...], pw[...], 1, 1) + product(avalue[...], av[...], 1, 1)
    ).astype(BF)


def expand(parts, pw, vv, av, vo, ao):
    tv, ta, (width, hd) = parts[0].shape[0], parts[3].shape[0], pw.shape
    step = min(512, width)
    small_v = pl.BlockSpec((tv, hd), lambda j: (0, 0))
    small_a = pl.BlockSpec((ta, hd), lambda j: (0, 0))
    tall = pl.BlockSpec((step, hd), lambda j: (j, 0))
    flat = pl.BlockSpec((hd, step), lambda j: (0, j))
    v_out = pl.BlockSpec((tv, step), lambda j: (0, j))
    a_out = pl.BlockSpec((ta, step), lambda j: (0, j))
    v_shape = jax.ShapeDtypeStruct((tv, width), BF)
    a_shape = jax.ShapeDtypeStruct((ta, width), BF)
    return pl.pallas_call(
        expand_kernel,
        grid=(width // step,),
        out_shape=(v_shape, a_shape, v_shape, a_shape),
        in_specs=[small_v] * 3 + [small_a] * 3 + [tall] * 3 + [flat] * 2,
        out_specs=(v_out, a_out, v_out, a_out),
    )(*parts, pw, vv, av, vo, ao)


def on_device(
    n_vid,
    n_aud,
    video_tokens,
    audio_tokens,
    pair_weight,
    video_value,
    audio_value,
    video_output,
    audio_output,
    video_cotangent,
    audio_cotangent,
):
    arrays = (
        video_tokens,
        audio_tokens,
        pair_weight,
        video_value,
        audio_value,
        video_output,
        audio_output,
        video_cotangent,
        audio_cotangent,
    )
    parts = attention_tile(
        n_vid, n_aud, video_tokens.shape[0], audio_tokens.shape[0], arrays
    )
    return expand(parts, pair_weight, video_value, audio_value, video_output, audio_output)


def solution(mesh):
    rows_v, rows_a = P(("vid", "aud"), None), P(("aud", "vid"), None)
    return jax.shard_map(
        functools.partial(on_device, mesh.shape["vid"], mesh.shape["aud"]),
        mesh=mesh,
        in_specs=(rows_v, rows_a, P(), P(), P(), P(), P(), rows_v, rows_a),
        out_specs=(rows_v, rows_a, rows_v, rows_a),
        check_vma=False,
    )
```

```python
import functools

import jax
import jax.numpy as jnp
from jax import lax
from jax.experimental import pallas as pl
from jax.experimental.pallas import tpu as pltpu
from jax.sharding import PartitionSpec as P

HS = 128
HEADS = 2
LANES = 128
MESH = pl.DeviceIdType.MESH
BF = jnp.bfloat16
F32 = jnp.float32


def product(left_side, right_side, left_dim, right_dim):
    return lax.dot_general(
        left_side,
        right_side,
        (((left_dim,), (right_dim,)), ((), ())),
        preferred_element_type=F32,
    )


def head_cols(head):
    return slice(head * HS, (head + 1) * HS)


def tile_kernel(
    n_vid,
    n_aud,
    vt_hbm,
    at_hbm,
    pw_hbm,
    vv_hbm,
    av_hbm,
    vo_hbm,
    ao_hbm,
    vc_hbm,
    ac_hbm,
    vmix_out,
    vpair_out,
    vvalue_out,
    amix_out,
    apair_out,
    avalue_out,
    vt,
    at,
    pw,
    vv,
    av,
    vo,
    ao,
    vc,
    ac,
    vblk,
    ablk,
    scores,
    colpeak,
    colsum,
    rstat,
    cstat,
    rfin,
    cfin,
    asum,
    vacc,
    vpart,
    vsib,
    vsum,
    vrecv,
    apart,
    arecv,
    load_sem,
    vg_send,
    vg_recv,
    vf_send,
    vf_recv,
    ag_send,
    ag_recv,
    rs_send,
    rs_recv,
    cs_send,
    cs_recv,
    vs_send,
    vs_recv,
    vr_send,
    vr_recv,
    ar_send,
    ar_recv,
):
    scale = float(HS) ** -0.5
    vid, aud = lax.axis_index("vid"), lax.axis_index("aud")
    n_chip = n_aud // 2
    core = lax.rem(aud, 2)
    chip = aud // 2
    sibling = aud + 1 - 2 * core
    tv, ta = vt.shape[0], at.shape[0]
    na = n_vid * ta
    half = n_vid // 2
    place = lax.rem(vid, half)
    near_base = vid - place
    far_base = half - near_base

    loads = {}
    for k, (name, src, dst) in enumerate(
        (
            ("at", at_hbm, at),
            ("pw", pw_hbm, pw),
            ("av", av_hbm, av),
            ("ac", ac_hbm, ac),
            ("ao", ao_hbm, ao),
            ("vt", vt_hbm, vt),
            ("vv", vv_hbm, vv),
            ("vc", vc_hbm, vc),
            ("vo", vo_hbm, vo),
        )
    ):
        loads[name] = pltpu.make_async_copy(src, dst, load_sem.at[k])
        loads[name].start()

    barrier = pltpu.get_barrier_semaphore()
    for d in range(1, n_aud):
        pl.semaphore_signal(
            barrier, inc=1, device_id={"aud": lax.rem(aud + d, n_aud)}, device_id_type=MESH
        )
    for d in range(1, n_vid):
        pl.semaphore_signal(
            barrier, inc=1, device_id={"vid": lax.rem(vid + d, n_vid)}, device_id_type=MESH
        )

    def remote(src, dst, send, recv, where):
        return pltpu.make_async_remote_copy(
            src_ref=src,
            dst_ref=dst,
            send_sem=send,
            recv_sem=recv,
            device_id=where,
            device_id_type=MESH,
        )

    pending = []

    def launch(copy):
        copy.start()
        pending.append(copy)
        return copy

    def project(blk, owner, p, left, right, right_dim):
        full = product(left[...], right[...], 1, right_dim).astype(BF)
        for head in range(HEADS):
            blk[head, owner, p] = full[:, head_cols(head)]

    def hop(head, way, s):
        owner = vid - s + 1 if way == 0 else vid + s - 1
        return remote(
            ablk.at[head, owner],
            ablk.at[head, owner],
            ag_send.at[head, way, s],
            ag_recv.at[head, way, s],
            {"vid": vid + 1 if way == 0 else vid - 1},
        )

    def sends(way, s):
        if way == 0:
            return (vid + 1 < n_vid) & (vid - s + 1 >= 0)
        return (vid > 0) & (vid + s - 1 < n_vid)

    def arrives(way, s):
        return vid - s >= 0 if way == 0 else vid + s < n_vid

    def audio_hop(head, s):
        for way in range(2):

            @pl.when(sends(way, s))
            def _(way=way):
                hop(head, way, s).start()

    def audio_take(head, s):
        for way in range(2):

            @pl.when(arrives(way, s))
            def _(way=way):
                hop(head, way, s).wait_recv()

        if s + 1 < n_vid:
            audio_hop(head, s + 1)

    loads["at"].wait()
    loads["pw"].wait()
    project(ablk, vid, 0, at, pw, 0)
    loads["av"].wait()
    project(ablk, vid, 1, at, av, 0)
    loads["ac"].wait()
    loads["ao"].wait()
    project(ablk, vid, 2, ac, ao, 1)
    pl.semaphore_wait(barrier, n_aud + n_vid - 2)
    for head in range(HEADS):
        audio_hop(head, 1)
    loads["vt"].wait()
    project(vblk, aud, 0, vt, pw, 0)
    loads["vv"].wait()
    project(vblk, aud, 1, vt, vv, 0)
    loads["vc"].wait()
    loads["vo"].wait()
    project(vblk, aud, 2, vc, vo, 1)
    v_copies, s_copies = {}, {}

    def share_own(head):
        for d in range(1, n_chip):
            v_copies[head, d] = launch(
                remote(
                    vblk.at[head, aud],
                    vblk.at[head, aud],
                    vg_send.at[head, d],
                    vg_recv.at[head, d],
                    {"aud": lax.rem(aud + 2 * d, n_aud)},
                )
            )
        s_copies[head, 0] = launch(
            remote(
                vblk.at[head, aud],
                vblk.at[head, aud],
                vf_send.at[head, 0],
                vf_recv.at[head, 0],
                {"aud": sibling},
            )
        )

    def video_take(head):
        for d in range(1, n_chip):
            v_copies[head, d].wait_recv()
            owner = lax.rem(aud + n_aud - 2 * d, n_aud)
            s_copies[head, d] = launch(
                remote(
                    vblk.at[head, owner],
                    vblk.at[head, owner],
                    vf_send.at[head, d],
                    vf_recv.at[head, d],
                    {"aud": sibling},
                )
            )

    def video_done(head):
        for d in range(n_chip):
            s_copies[head, d].wait_recv()

    def audio_side(p, head):
        return ablk[head, :, p].reshape(na, HS)

    for head in range(HEADS):
        share_own(head)
    audio_take(0, 1)
    video_take(0)
    for s in range(2, n_vid):
        audio_take(0, s)
    video_done(0)

    lane = lax.broadcasted_iota(jnp.int32, (tv, LANES), 1)
    sub = lax.broadcasted_iota(jnp.int32, (LANES, tv), 0)
    stat_copies = {0: [], 1: []}
    for head in range(HEADS):
        apairs, avalues, aback = (audio_side(p, head) for p in range(3))
        colpeak[head] = jnp.full((8, na), -jnp.inf, F32)

        def score_step(i, carry, head=head, apairs=apairs):
            s = scale * product(vblk[head, i, 0], apairs, 1, 1)
            scores[head, i] = s
            colpeak[head] = jnp.maximum(
                colpeak[head], jnp.max(s.reshape(tv // 8, 8, na), axis=0)
            )
            return carry

        lax.fori_loop(0, n_aud, score_step, 0)
        if head + 1 < HEADS:
            audio_take(head + 1, 1)
            video_take(head + 1)
        peak = jnp.max(colpeak[head], axis=0, keepdims=True)
        colsum[...] = jnp.zeros_like(colsum)

        def stat_step(i, carry, head=head, avalues=avalues, aback=aback, peak=peak):
            s = scores[head, i]
            row_peak = jnp.max(s, axis=1, keepdims=True)
            row_exp = jnp.exp(s - row_peak)
            col_exp = jnp.exp(s - peak)
            row_grad = product(vblk[head, i, 2], avalues, 1, 1)
            col_grad = product(vblk[head, i, 1], aback, 1, 1)
            row_total = jnp.sum(row_exp, axis=1, keepdims=True)
            row_dot = jnp.sum(row_exp * row_grad, axis=1, keepdims=True)
            colsum[0] += jnp.sum(col_exp.reshape(tv // 8, 8, na), axis=0)
            colsum[1] += jnp.sum((col_exp * col_grad).reshape(tv // 8, 8, na), axis=0)
            packed = jnp.where(lane == 0, row_peak, jnp.where(lane == 1, row_total, row_dot)).T
            for k in range(3):
                rstat[head, 0, k, pl.ds(i, 1), :] = packed[k : k + 1]
            return carry

        if head + 1 < HEADS:
            steps = max(n_vid - 2, 1)
            for k in range(steps):
                lax.fori_loop(k * n_aud // steps, (k + 1) * n_aud // steps, stat_step, 0)
                if k + 2 < n_vid:
                    audio_take(head + 1, k + 2)
        else:
            lax.fori_loop(0, n_aud, stat_step, 0)
        cstat[head, 0, 0:1] = peak
        for k in range(2):
            cstat[head, 0, k + 1 : k + 2] = jnp.sum(colsum[k], axis=0, keepdims=True)
        for d in range(1, n_aud):
            stat_copies[head].append(
                launch(
                    remote(
                        rstat.at[head, 0],
                        rstat.at[head, d],
                        rs_send.at[head, d],
                        rs_recv.at[head, d],
                        {"aud": lax.rem(aud + d, n_aud)},
                    )
                )
            )
        for d in range(1, n_vid):
            stat_copies[head].append(
                launch(
                    remote(
                        cstat.at[head, 0],
                        cstat.at[head, d],
                        cs_send.at[head, d],
                        cs_recv.at[head, d],
                        {"vid": lax.rem(vid + d, n_vid)},
                    )
                )
            )

        if head + 1 < HEADS:
            video_done(head + 1)

    def combine(parts):
        top = functools.reduce(jnp.maximum, [part[0] for part in parts])
        gains = [jnp.exp(part[0] - top) for part in parts]
        total = sum(part[1] * gain for part, gain in zip(parts, gains))
        dots = sum(part[2] * gain for part, gain in zip(parts, gains))
        return top, 1.0 / total, dots / total

    sib_copies, vr_copies, ar_copies = {}, {}, {}

    def reduce_video(head):
        sib_copies[head].wait_recv()
        for d in range(1, n_chip):
            peer = lax.rem(chip + d, n_chip)
            vsum[head, d] = (
                vpart[head, core, peer].astype(F32) + vsib[head, peer].astype(F32)
            ).astype(BF)
            vr_copies[head, d] = launch(
                remote(
                    vsum.at[head, d],
                    vrecv.at[head, d],
                    vr_send.at[head, d],
                    vr_recv.at[head, d],
                    {"aud": lax.rem(aud + 2 * d, n_aud)},
                )
            )

    for head in range(HEADS):
        for copy in stat_copies[head]:
            copy.wait_recv()
        for k, value in enumerate(
            combine([[rstat[head, d, k] for k in range(3)] for d in range(n_aud)])
        ):
            rfin[k] = value
        for k, value in enumerate(
            combine([[cstat[head, d, k : k + 1] for k in range(3)] for d in range(n_vid)])
        ):
            cfin[k : k + 1] = value
        for turn in range(2):
            base = (far_base, near_base)[turn]
            cols = pl.ds(pl.multiple_of(base * ta, LANES), half * ta)
            apairs, avalues, aback = (
                ablk[head, pl.ds(base, half), p].reshape(half * ta, HS) for p in range(3)
            )
            col_fin = [cfin[k : k + 1, cols] for k in range(3)]
            asum[...] = jnp.zeros_like(asum)

            def grad_step(
                i,
                carry,
                head=head,
                turn=turn,
                cols=cols,
                apairs=apairs,
                avalues=avalues,
                aback=aback,
                col_fin=col_fin,
            ):
                rows = [rfin[k, pl.ds(i, 1), :] for k in range(3)]
                back = jnp.where(sub == 0, rows[0], jnp.where(sub == 1, rows[1], rows[2])).T
                s = scores[head, i, :, cols]
                vpairs = vblk[head, i, 0]
                vvalues = vblk[head, i, 1]
                vback = vblk[head, i, 2]
                row_prob = jnp.exp(s - back[:, 0:1]) * back[:, 1:2]
                col_prob = jnp.exp(s - col_fin[0]) * col_fin[1]
                row_weight, col_weight = row_prob.astype(BF), col_prob.astype(BF)
                row_grad = product(vback, avalues, 1, 1)
                col_grad = product(vvalues, aback, 1, 1)
                score_grad = (
                    row_prob * (row_grad - back[:, 2:3]) + col_prob * (col_grad - col_fin[2])
                ).astype(BF)
                terms = (
                    product(row_weight, avalues, 1, 0),
                    scale * product(score_grad, apairs, 1, 0),
                    product(col_weight, aback, 1, 0),
                )
                for k in range(3):
                    if turn == 0:
                        vacc[i, :, head_cols(k)] = terms[k]
                    else:
                        vpart[head, lax.rem(i, 2), i // 2, :, head_cols(k)] = (
                            vacc[i, :, head_cols(k)] + terms[k]
                        ).astype(BF)
                asum[:, 0:HS] += product(col_weight, vvalues, 0, 0)
                asum[:, HS : 2 * HS] += product(score_grad, vpairs, 0, 0)
                asum[:, 2 * HS : 3 * HS] += product(row_weight, vback, 0, 0)
                return carry

            lax.fori_loop(0, n_aud, grad_step, 0)
            for t in range(half):
                rows = slice(t * ta, (t + 1) * ta)
                apart[head, base + t, :, 0:HS] = asum[rows, 0:HS].astype(BF)
                apart[head, base + t, :, HS : 2 * HS] = (
                    scale * asum[rows, HS : 2 * HS]
                ).astype(BF)
                apart[head, base + t, :, 2 * HS : 3 * HS] = asum[rows, 2 * HS : 3 * HS].astype(BF)
            for d in range(turn, half):
                peer = base + lax.rem(place + d, half)
                slot = d if turn == 0 else half - 1 + d
                ar_copies[head, slot] = launch(
                    remote(
                        apart.at[head, peer],
                        arecv.at[head, slot],
                        ar_send.at[head, slot],
                        ar_recv.at[head, slot],
                        {"vid": peer},
                    )
                )
        sib_copies[head] = launch(
            remote(
                vpart.at[head, 1 - core],
                vsib.at[head],
                vs_send.at[head],
                vs_recv.at[head],
                {"aud": sibling},
            )
        )
        if head > 0:
            reduce_video(head - 1)
    reduce_video(HEADS - 1)

    v_out = (vmix_out, vpair_out, vvalue_out)
    a_out = (amix_out, apair_out, avalue_out)
    for head in range(HEADS):
        for d in range(1, n_chip):
            vr_copies[head, d].wait_recv()
        total = vpart[head, core, chip].astype(F32) + vsib[head, chip].astype(F32)
        for d in range(1, n_chip):
            total += vrecv[head, d].astype(F32)
        for k in range(3):
            v_out[k][:, head_cols(head)] = total[:, head_cols(k)].astype(BF)
        for d in range(n_vid - 1):
            ar_copies[head, d].wait_recv()
        total = apart[head, vid].astype(F32)
        for d in range(n_vid - 1):
            total += arecv[head, d].astype(F32)
        for k in range(3):
            a_out[k][:, head_cols(head)] = total[:, head_cols(k)].astype(BF)
    for head in range(HEADS):
        for way in range(2):
            for s in range(1, n_vid):

                @pl.when(sends(way, s))
                def _(head=head, way=way, s=s):
                    hop(head, way, s).wait_send()

    for copy in pending:
        copy.wait_send()


def attention_tile(n_vid, n_aud, tv, ta, arrays):
    nv, na = n_aud * tv, n_vid * ta
    n_chip = n_aud // 2
    wide = 3 * HS
    dma = pltpu.SemaphoreType.DMA
    v_shape = jax.ShapeDtypeStruct((tv, HEADS * HS), BF)
    a_shape = jax.ShapeDtypeStruct((ta, HEADS * HS), BF)
    sems = [
        (HEADS, n_chip),
        (HEADS, n_chip),
        (HEADS, 2, n_vid),
        (HEADS, n_aud),
        (HEADS, n_vid),
        (HEADS,),
        (HEADS, n_chip),
        (HEADS, n_vid),
    ]
    return pl.pallas_call(
        functools.partial(tile_kernel, n_vid, n_aud),
        out_shape=(v_shape,) * 3 + (a_shape,) * 3,
        in_specs=[pl.BlockSpec(memory_space=pl.ANY)] * 9,
        out_specs=(pl.BlockSpec(memory_space=pltpu.VMEM),) * 6,
        scratch_shapes=[pltpu.VMEM(array.shape, BF) for array in arrays]
        + [
            pltpu.VMEM((HEADS, n_aud, 3, tv, HS), BF),
            pltpu.VMEM((HEADS, n_vid, 3, ta, HS), BF),
            pltpu.VMEM((HEADS, n_aud, tv, na), F32),
            pltpu.VMEM((HEADS, 8, na), F32),
            pltpu.VMEM((2, 8, na), F32),
            pltpu.VMEM((HEADS, n_aud, 3, n_aud, LANES), F32),
            pltpu.VMEM((HEADS, n_vid, 3, na), F32),
            pltpu.VMEM((3, n_aud, LANES), F32),
            pltpu.VMEM((3, na), F32),
            pltpu.VMEM((na // 2, wide), F32),
            pltpu.VMEM((n_aud, tv, wide), F32),
            pltpu.VMEM((HEADS, 2, n_chip, tv, wide), BF),
            pltpu.VMEM((HEADS, n_chip, tv, wide), BF),
            pltpu.VMEM((HEADS, n_chip, tv, wide), BF),
            pltpu.VMEM((HEADS, n_chip, tv, wide), BF),
            pltpu.VMEM((HEADS, n_vid, ta, wide), BF),
            pltpu.VMEM((HEADS, n_vid, ta, wide), BF),
        ]
        + [dma((len(arrays),))]
        + [dma(shape) for shape in sems for _ in range(2)],
        compiler_params=pltpu.CompilerParams(
            collective_id=0, has_side_effects=True, vmem_limit_bytes=63 * 1024 * 1024
        ),
    )(*arrays)


def on_device(
    n_vid,
    n_aud,
    video_tokens,
    audio_tokens,
    pair_weight,
    video_value,
    audio_value,
    video_output,
    audio_output,
    video_cotangent,
    audio_cotangent,
):
    arrays = (
        video_tokens,
        audio_tokens,
        pair_weight,
        video_value,
        audio_value,
        video_output,
        audio_output,
        video_cotangent,
        audio_cotangent,
    )
    vmix, vpair, vvalue, amix, apair, avalue = attention_tile(
        n_vid, n_aud, video_tokens.shape[0], audio_tokens.shape[0], arrays
    )
    video_result = product(vmix, video_output, 1, 0).astype(BF)
    audio_result = product(amix, audio_output, 1, 0).astype(BF)
    video_gradient = (
        product(vpair, pair_weight, 1, 1) + product(vvalue, video_value, 1, 1)
    ).astype(BF)
    audio_gradient = (
        product(apair, pair_weight, 1, 1) + product(avalue, audio_value, 1, 1)
    ).astype(BF)
    return (video_result, audio_result, video_gradient, audio_gradient)


def solution(mesh):
    rows_v, rows_a = P(("vid", "aud"), None), P(("aud", "vid"), None)
    return jax.shard_map(
        functools.partial(on_device, mesh.shape["vid"], mesh.shape["aud"]),
        mesh=mesh,
        in_specs=(rows_v, rows_a, P(), P(), P(), P(), P(), rows_v, rows_a),
        out_specs=(rows_v, rows_a, rows_v, rows_a),
        check_vma=False,
    )
```

```python
import functools

import jax
import jax.numpy as jnp
from jax import lax
from jax.experimental import pallas as pl
from jax.experimental.pallas import tpu as pltpu
from jax.sharding import PartitionSpec as P

HS = 128
HEADS = 2
LANES = 128
MESH = pl.DeviceIdType.MESH
BF = jnp.bfloat16
F32 = jnp.float32


def product(left_side, right_side, left_dim, right_dim):
    return lax.dot_general(
        left_side,
        right_side,
        (((left_dim,), (right_dim,)), ((), ())),
        preferred_element_type=F32,
    )


def head_cols(head):
    return slice(head * HS, (head + 1) * HS)


def tile_kernel(
    n_vid,
    n_aud,
    vt_hbm,
    at_hbm,
    pw_hbm,
    vv_hbm,
    av_hbm,
    vo_hbm,
    ao_hbm,
    vc_hbm,
    ac_hbm,
    vmix_out,
    vpair_out,
    vvalue_out,
    amix_out,
    apair_out,
    avalue_out,
    vt,
    at,
    pw,
    vv,
    av,
    vo,
    ao,
    vc,
    ac,
    vblk,
    ablk,
    scores,
    colpeak,
    colsum,
    rstat,
    cstat,
    rfin,
    cfin,
    asum,
    vpart,
    vsib,
    vsum,
    vrecv,
    apart,
    arecv,
    load_sem,
    vg_send,
    vg_recv,
    vf_send,
    vf_recv,
    ag_send,
    ag_recv,
    rs_send,
    rs_recv,
    cs_send,
    cs_recv,
    vs_send,
    vs_recv,
    vr_send,
    vr_recv,
    ar_send,
    ar_recv,
):
    scale = float(HS) ** -0.5
    vid, aud = lax.axis_index("vid"), lax.axis_index("aud")
    n_chip = n_aud // 2
    core = lax.rem(aud, 2)
    chip = aud // 2
    sibling = aud + 1 - 2 * core
    tv, ta = vt.shape[0], at.shape[0]
    na = n_vid * ta

    loads = {}
    for k, (name, src, dst) in enumerate(
        (
            ("at", at_hbm, at),
            ("pw", pw_hbm, pw),
            ("av", av_hbm, av),
            ("ac", ac_hbm, ac),
            ("ao", ao_hbm, ao),
            ("vt", vt_hbm, vt),
            ("vv", vv_hbm, vv),
            ("vc", vc_hbm, vc),
            ("vo", vo_hbm, vo),
        )
    ):
        loads[name] = pltpu.make_async_copy(src, dst, load_sem.at[k])
        loads[name].start()

    barrier = pltpu.get_barrier_semaphore()
    for d in range(1, n_aud):
        pl.semaphore_signal(
            barrier, inc=1, device_id={"aud": lax.rem(aud + d, n_aud)}, device_id_type=MESH
        )
    for d in range(1, n_vid):
        pl.semaphore_signal(
            barrier, inc=1, device_id={"vid": lax.rem(vid + d, n_vid)}, device_id_type=MESH
        )

    def remote(src, dst, send, recv, where):
        return pltpu.make_async_remote_copy(
            src_ref=src,
            dst_ref=dst,
            send_sem=send,
            recv_sem=recv,
            device_id=where,
            device_id_type=MESH,
        )

    pending = []

    def launch(copy):
        copy.start()
        pending.append(copy)
        return copy

    def project(blk, owner, p, left, right, right_dim):
        full = product(left[...], right[...], 1, right_dim).astype(BF)
        for head in range(HEADS):
            blk[head, owner, p] = full[:, head_cols(head)]

    def hop(head, way, s):
        owner = vid - s + 1 if way == 0 else vid + s - 1
        return remote(
            ablk.at[head, owner],
            ablk.at[head, owner],
            ag_send.at[head, way, s],
            ag_recv.at[head, way, s],
            {"vid": vid + 1 if way == 0 else vid - 1},
        )

    def sends(way, s):
        if way == 0:
            return (vid + 1 < n_vid) & (vid - s + 1 >= 0)
        return (vid > 0) & (vid + s - 1 < n_vid)

    def arrives(way, s):
        return vid - s >= 0 if way == 0 else vid + s < n_vid

    def audio_hop(head, s):
        for way in range(2):

            @pl.when(sends(way, s))
            def _(way=way):
                hop(head, way, s).start()

    def audio_take(head, s):
        for way in range(2):

            @pl.when(arrives(way, s))
            def _(way=way):
                hop(head, way, s).wait_recv()

        if s + 1 < n_vid:
            audio_hop(head, s + 1)

    loads["at"].wait()
    loads["pw"].wait()
    project(ablk, vid, 0, at, pw, 0)
    loads["av"].wait()
    project(ablk, vid, 1, at, av, 0)
    loads["ac"].wait()
    loads["ao"].wait()
    project(ablk, vid, 2, ac, ao, 1)
    pl.semaphore_wait(barrier, n_aud + n_vid - 2)
    for head in range(HEADS):
        audio_hop(head, 1)
    loads["vt"].wait()
    project(vblk, aud, 0, vt, pw, 0)
    loads["vv"].wait()
    project(vblk, aud, 1, vt, vv, 0)
    loads["vc"].wait()
    loads["vo"].wait()
    project(vblk, aud, 2, vc, vo, 1)
    v_copies, s_copies = {}, {}

    def share_own(head):
        for d in range(1, n_chip):
            v_copies[head, d] = launch(
                remote(
                    vblk.at[head, aud],
                    vblk.at[head, aud],
                    vg_send.at[head, d],
                    vg_recv.at[head, d],
                    {"aud": lax.rem(aud + 2 * d, n_aud)},
                )
            )
        s_copies[head, 0] = launch(
            remote(
                vblk.at[head, aud],
                vblk.at[head, aud],
                vf_send.at[head, 0],
                vf_recv.at[head, 0],
                {"aud": sibling},
            )
        )

    def video_take(head):
        for d in range(1, n_chip):
            v_copies[head, d].wait_recv()
            owner = lax.rem(aud + n_aud - 2 * d, n_aud)
            s_copies[head, d] = launch(
                remote(
                    vblk.at[head, owner],
                    vblk.at[head, owner],
                    vf_send.at[head, d],
                    vf_recv.at[head, d],
                    {"aud": sibling},
                )
            )

    def video_done(head):
        for d in range(n_chip):
            s_copies[head, d].wait_recv()

    def audio_side(p, head):
        return ablk[head, :, p].reshape(na, HS)

    for head in range(HEADS):
        share_own(head)
    audio_take(0, 1)
    video_take(0)
    for s in range(2, n_vid):
        audio_take(0, s)
    video_done(0)

    lane = lax.broadcasted_iota(jnp.int32, (tv, LANES), 1)
    sub = lax.broadcasted_iota(jnp.int32, (LANES, tv), 0)
    stat_copies = {0: [], 1: []}
    for head in range(HEADS):
        apairs, avalues, aback = (audio_side(p, head) for p in range(3))
        colpeak[head] = jnp.full((8, na), -jnp.inf, F32)

        def score_step(i, carry, head=head, apairs=apairs):
            s = scale * product(vblk[head, i, 0], apairs, 1, 1)
            scores[head, i] = s
            colpeak[head] = jnp.maximum(
                colpeak[head], jnp.max(s.reshape(tv // 8, 8, na), axis=0)
            )
            return carry

        lax.fori_loop(0, n_aud, score_step, 0)
        if head + 1 < HEADS:
            audio_take(head + 1, 1)
            video_take(head + 1)
        peak = jnp.max(colpeak[head], axis=0, keepdims=True)
        colsum[...] = jnp.zeros_like(colsum)

        def stat_step(i, carry, head=head, avalues=avalues, aback=aback, peak=peak):
            s = scores[head, i]
            row_peak = jnp.max(s, axis=1, keepdims=True)
            row_exp = jnp.exp(s - row_peak)
            col_exp = jnp.exp(s - peak)
            row_grad = product(vblk[head, i, 2], avalues, 1, 1)
            col_grad = product(vblk[head, i, 1], aback, 1, 1)
            row_total = jnp.sum(row_exp, axis=1, keepdims=True)
            row_dot = jnp.sum(row_exp * row_grad, axis=1, keepdims=True)
            colsum[0] += jnp.sum(col_exp.reshape(tv // 8, 8, na), axis=0)
            colsum[1] += jnp.sum((col_exp * col_grad).reshape(tv // 8, 8, na), axis=0)
            packed = jnp.where(lane == 0, row_peak, jnp.where(lane == 1, row_total, row_dot)).T
            for k in range(3):
                rstat[head, 0, k, pl.ds(i, 1), :] = packed[k : k + 1]
            return carry

        if head + 1 < HEADS:
            steps = max(n_vid - 2, 1)
            for k in range(steps):
                lax.fori_loop(k * n_aud // steps, (k + 1) * n_aud // steps, stat_step, 0)
                if k + 2 < n_vid:
                    audio_take(head + 1, k + 2)
        else:
            lax.fori_loop(0, n_aud, stat_step, 0)
        cstat[head, 0, 0:1] = peak
        for k in range(2):
            cstat[head, 0, k + 1 : k + 2] = jnp.sum(colsum[k], axis=0, keepdims=True)
        for d in range(1, n_aud):
            stat_copies[head].append(
                launch(
                    remote(
                        rstat.at[head, 0],
                        rstat.at[head, d],
                        rs_send.at[head, d],
                        rs_recv.at[head, d],
                        {"aud": lax.rem(aud + d, n_aud)},
                    )
                )
            )
        for d in range(1, n_vid):
            stat_copies[head].append(
                launch(
                    remote(
                        cstat.at[head, 0],
                        cstat.at[head, d],
                        cs_send.at[head, d],
                        cs_recv.at[head, d],
                        {"vid": lax.rem(vid + d, n_vid)},
                    )
                )
            )

        if head + 1 < HEADS:
            video_done(head + 1)

    def combine(parts):
        top = functools.reduce(jnp.maximum, [part[0] for part in parts])
        gains = [jnp.exp(part[0] - top) for part in parts]
        total = sum(part[1] * gain for part, gain in zip(parts, gains))
        dots = sum(part[2] * gain for part, gain in zip(parts, gains))
        return top, 1.0 / total, dots / total

    sib_copies, vr_copies, ar_copies = {}, {}, {}

    def reduce_video(head):
        sib_copies[head].wait_recv()
        for d in range(1, n_chip):
            peer = lax.rem(chip + d, n_chip)
            vsum[head, d] = (
                vpart[head, core, peer].astype(F32) + vsib[head, peer].astype(F32)
            ).astype(BF)
            vr_copies[head, d] = launch(
                remote(
                    vsum.at[head, d],
                    vrecv.at[head, d],
                    vr_send.at[head, d],
                    vr_recv.at[head, d],
                    {"aud": lax.rem(aud + 2 * d, n_aud)},
                )
            )

    for head in range(HEADS):
        for copy in stat_copies[head]:
            copy.wait_recv()
        for k, value in enumerate(
            combine([[rstat[head, d, k] for k in range(3)] for d in range(n_aud)])
        ):
            rfin[k] = value
        for k, value in enumerate(
            combine([[cstat[head, d, k : k + 1] for k in range(3)] for d in range(n_vid)])
        ):
            cfin[k : k + 1] = value
        apairs, avalues, aback = (audio_side(p, head) for p in range(3))
        asum[...] = jnp.zeros_like(asum)

        def grad_step(i, carry, head=head, apairs=apairs, avalues=avalues, aback=aback):
            rows = [rfin[k, pl.ds(i, 1), :] for k in range(3)]
            back = jnp.where(sub == 0, rows[0], jnp.where(sub == 1, rows[1], rows[2])).T
            s = scores[head, i]
            vpairs = vblk[head, i, 0]
            vvalues = vblk[head, i, 1]
            vback = vblk[head, i, 2]
            row_prob = jnp.exp(s - back[:, 0:1]) * back[:, 1:2]
            col_prob = jnp.exp(s - cfin[0:1]) * cfin[1:2]
            row_weight, col_weight = row_prob.astype(BF), col_prob.astype(BF)
            row_grad = product(vback, avalues, 1, 1)
            col_grad = product(vvalues, aback, 1, 1)
            score_grad = (
                row_prob * (row_grad - back[:, 2:3]) + col_prob * (col_grad - cfin[2:3])
            ).astype(BF)
            slot = (head, lax.rem(i, 2), i // 2)
            vpart[slot + (slice(None), slice(0, HS))] = product(row_weight, avalues, 1, 0).astype(BF)
            vpart[slot + (slice(None), slice(HS, 2 * HS))] = (
                scale * product(score_grad, apairs, 1, 0)
            ).astype(BF)
            vpart[slot + (slice(None), slice(2 * HS, 3 * HS))] = product(
                col_weight, aback, 1, 0
            ).astype(BF)
            asum[:, 0:HS] += product(col_weight, vvalues, 0, 0)
            asum[:, HS : 2 * HS] += product(score_grad, vpairs, 0, 0)
            asum[:, 2 * HS : 3 * HS] += product(row_weight, vback, 0, 0)
            return carry

        lax.fori_loop(0, n_aud, grad_step, 0)
        for t in range(n_vid):
            rows = slice(t * ta, (t + 1) * ta)
            apart[head, t, :, 0:HS] = asum[rows, 0:HS].astype(BF)
            apart[head, t, :, HS : 2 * HS] = (scale * asum[rows, HS : 2 * HS]).astype(BF)
            apart[head, t, :, 2 * HS : 3 * HS] = asum[rows, 2 * HS : 3 * HS].astype(BF)
        for d in range(1, n_vid):
            peer = lax.rem(vid + d, n_vid)
            ar_copies[head, d] = launch(
                remote(
                    apart.at[head, peer],
                    arecv.at[head, d],
                    ar_send.at[head, d],
                    ar_recv.at[head, d],
                    {"vid": peer},
                )
            )
        sib_copies[head] = launch(
            remote(
                vpart.at[head, 1 - core],
                vsib.at[head],
                vs_send.at[head],
                vs_recv.at[head],
                {"aud": sibling},
            )
        )
        if head > 0:
            reduce_video(head - 1)
    reduce_video(HEADS - 1)

    v_out = (vmix_out, vpair_out, vvalue_out)
    a_out = (amix_out, apair_out, avalue_out)
    for head in range(HEADS):
        for d in range(1, n_chip):
            vr_copies[head, d].wait_recv()
        total = vpart[head, core, chip].astype(F32) + vsib[head, chip].astype(F32)
        for d in range(1, n_chip):
            total += vrecv[head, d].astype(F32)
        for k in range(3):
            v_out[k][:, head_cols(head)] = total[:, head_cols(k)].astype(BF)
        for d in range(1, n_vid):
            ar_copies[head, d].wait_recv()
        total = apart[head, vid].astype(F32)
        for d in range(1, n_vid):
            total += arecv[head, d].astype(F32)
        for k in range(3):
            a_out[k][:, head_cols(head)] = total[:, head_cols(k)].astype(BF)
    for head in range(HEADS):
        for way in range(2):
            for s in range(1, n_vid):

                @pl.when(sends(way, s))
                def _(head=head, way=way, s=s):
                    hop(head, way, s).wait_send()

    for copy in pending:
        copy.wait_send()


def attention_tile(n_vid, n_aud, tv, ta, arrays):
    nv, na = n_aud * tv, n_vid * ta
    n_chip = n_aud // 2
    wide = 3 * HS
    dma = pltpu.SemaphoreType.DMA
    v_shape = jax.ShapeDtypeStruct((tv, HEADS * HS), BF)
    a_shape = jax.ShapeDtypeStruct((ta, HEADS * HS), BF)
    sems = [
        (HEADS, n_chip),
        (HEADS, n_chip),
        (HEADS, 2, n_vid),
        (HEADS, n_aud),
        (HEADS, n_vid),
        (HEADS,),
        (HEADS, n_chip),
        (HEADS, n_vid),
    ]
    return pl.pallas_call(
        functools.partial(tile_kernel, n_vid, n_aud),
        out_shape=(v_shape,) * 3 + (a_shape,) * 3,
        in_specs=[pl.BlockSpec(memory_space=pl.ANY)] * 9,
        out_specs=(pl.BlockSpec(memory_space=pltpu.VMEM),) * 6,
        scratch_shapes=[pltpu.VMEM(array.shape, BF) for array in arrays]
        + [
            pltpu.VMEM((HEADS, n_aud, 3, tv, HS), BF),
            pltpu.VMEM((HEADS, n_vid, 3, ta, HS), BF),
            pltpu.VMEM((HEADS, n_aud, tv, na), F32),
            pltpu.VMEM((HEADS, 8, na), F32),
            pltpu.VMEM((2, 8, na), F32),
            pltpu.VMEM((HEADS, n_aud, 3, n_aud, LANES), F32),
            pltpu.VMEM((HEADS, n_vid, 3, na), F32),
            pltpu.VMEM((3, n_aud, LANES), F32),
            pltpu.VMEM((3, na), F32),
            pltpu.VMEM((na, wide), F32),
            pltpu.VMEM((HEADS, 2, n_chip, tv, wide), BF),
            pltpu.VMEM((HEADS, n_chip, tv, wide), BF),
            pltpu.VMEM((HEADS, n_chip, tv, wide), BF),
            pltpu.VMEM((HEADS, n_chip, tv, wide), BF),
            pltpu.VMEM((HEADS, n_vid, ta, wide), BF),
            pltpu.VMEM((HEADS, n_vid, ta, wide), BF),
        ]
        + [dma((len(arrays),))]
        + [dma(shape) for shape in sems for _ in range(2)],
        compiler_params=pltpu.CompilerParams(
            collective_id=0, has_side_effects=True, vmem_limit_bytes=63 * 1024 * 1024
        ),
    )(*arrays)


def expand_kernel(
    vmix, vpair, vvalue, amix, apair, avalue, pw, vv, av, vo, ao, vres, ares, vgrad, agrad
):
    vres[...] = product(vmix[...], vo[...], 1, 0).astype(BF)
    ares[...] = product(amix[...], ao[...], 1, 0).astype(BF)
    vgrad[...] = (
        product(vpair[...], pw[...], 1, 1) + product(vvalue[...], vv[...], 1, 1)
    ).astype(BF)
    agrad[...] = (
        product(apair[...], pw[...], 1, 1) + product(avalue[...], av[...], 1, 1)
    ).astype(BF)


def expand(parts, pw, vv, av, vo, ao):
    tv, ta, (width, hd) = parts[0].shape[0], parts[3].shape[0], pw.shape
    step = min(1024, width)
    small_v = pl.BlockSpec((tv, hd), lambda j: (0, 0))
    small_a = pl.BlockSpec((ta, hd), lambda j: (0, 0))
    tall = pl.BlockSpec((step, hd), lambda j: (j, 0))
    flat = pl.BlockSpec((hd, step), lambda j: (0, j))
    v_out = pl.BlockSpec((tv, step), lambda j: (0, j))
    a_out = pl.BlockSpec((ta, step), lambda j: (0, j))
    v_shape = jax.ShapeDtypeStruct((tv, width), BF)
    a_shape = jax.ShapeDtypeStruct((ta, width), BF)
    return pl.pallas_call(
        expand_kernel,
        grid=(width // step,),
        out_shape=(v_shape, a_shape, v_shape, a_shape),
        in_specs=[small_v] * 3 + [small_a] * 3 + [tall] * 3 + [flat] * 2,
        out_specs=(v_out, a_out, v_out, a_out),
    )(*parts, pw, vv, av, vo, ao)


def on_device(
    n_vid,
    n_aud,
    video_tokens,
    audio_tokens,
    pair_weight,
    video_value,
    audio_value,
    video_output,
    audio_output,
    video_cotangent,
    audio_cotangent,
):
    arrays = (
        video_tokens,
        audio_tokens,
        pair_weight,
        video_value,
        audio_value,
        video_output,
        audio_output,
        video_cotangent,
        audio_cotangent,
    )
    parts = attention_tile(
        n_vid, n_aud, video_tokens.shape[0], audio_tokens.shape[0], arrays
    )
    return expand(parts, pair_weight, video_value, audio_value, video_output, audio_output)


def solution(mesh):
    rows_v, rows_a = P(("vid", "aud"), None), P(("aud", "vid"), None)
    return jax.shard_map(
        functools.partial(on_device, mesh.shape["vid"], mesh.shape["aud"]),
        mesh=mesh,
        in_specs=(rows_v, rows_a, P(), P(), P(), P(), P(), rows_v, rows_a),
        out_specs=(rows_v, rows_a, rows_v, rows_a),
        check_vma=False,
    )
```
